32 devices in a mesh: rows: 8 (over y, x, core), chan: 4 (over z).
Axes of the slice: x: 2, y: 2, z: 4, core: 2. Of those that a mesh axis runs over, the one named last changes fastest.
Arguments:
- latents: bfloat16 [512, 4, 8, 128], P('chan', None, 'rows'), may hold values from -20 to 20
- cache_one: bfloat16 [512, 2, 8, 128], P('chan', None, 'rows'), may hold values from -4 to 4
- cache_two: bfloat16 [512, 2, 8, 128], P('chan', None, 'rows'), may hold values from -4 to 4
- gain_one: float32 [512], P('chan'), may hold values from 0.25 to 1.75
- bias_one: float32 [512], P('chan'), may hold values from -0.8 to 0.8
- weight_one: bfloat16 [3, 3, 3, 512, 512], P(None, None, None, None, 'chan'), may hold values from -0.0546875 to 0.0546875
- gain_two: float32 [512], P('chan'), may hold values from 0.25 to 1.75
- bias_two: float32 [512], P('chan'), may hold values from -0.8 to 0.8
- weight_two: bfloat16 [3, 3, 3, 512, 512], P(None, None, None, 'chan'), may hold values from -0.0625 to 0.0625
Outputs:
- upsampled: float32 [512, 4, 16, 256], P('chan', None, 'rows')
The draws below stay inside these ranges and needn't reach their ends.
All inputs are finite; a program needn't handle non-finite values.
Results may differ from the reference program's by a relative error of at most 0.0022.
Values may be sent and summed in bfloat16 or wider, within the bound.
A program may use at most 64 MiB of HBM per device.

```python
import jax
import jax.numpy as jnp
from jax import lax

CHANNELS = 512
GROUPS = 32
FRAMES = 4
WIDTH = 128
HEIGHT = 8


def draw_latents(key, part):
    folded = jax.random.fold_in(key, 7)
    jitter_key, chan_key = jax.random.split(folded, 2)
    extent = (CHANNELS, FRAMES, HEIGHT, WIDTH)
    heights = jnp.arange(HEIGHT, dtype=jnp.float32) / (HEIGHT - 1)
    chan_scale = jnp.exp(jax.random.uniform(chan_key, (CHANNELS,), jnp.float32, -0.69, 0.69))
    jitter = jnp.clip(jax.random.normal(jitter_key, extent, jnp.float32), -3.0, 3.0)
    row_scale = 0.3 * 10.0 ** heights
    return (jitter * row_scale[None, None, :, None] * chan_scale[:, None, None, None]).astype(jnp.bfloat16)


def strengthened(drawn, rng, source, target, shards_of, factor):
    def block_of(axis_at):
        return (jnp.arange(drawn.shape[axis_at]) // (drawn.shape[axis_at] // shards_of)).reshape((-1,) + (1,) * (drawn.ndim - 1 - axis_at))

    near = jax.random.permutation(rng, shards_of)[block_of(target)]
    other_side = (block_of(target) + shards_of // 2) % shards_of
    return jnp.where((block_of(source) == near) | (block_of(source) == other_side), factor * drawn, drawn)


def block_scale(own_key, dims, pieces, least, top_value):
    def one(dim, shards_of):
        steps = jax.random.uniform(jax.random.fold_in(jax.random.fold_in(own_key, 6), dim), (shards_of,), jnp.float32, least / len(pieces), top_value / len(pieces))
        return jnp.repeat(jnp.exp(steps), dims[dim] // shards_of).reshape((-1,) + (1,) * (len(dims) - dim - 1))

    loudness = one(*pieces[0])
    for cut in pieces[1:]:
        loudness = loudness * one(*cut)
    return loudness


def scatter_about(rng, dims, deviation, bound, shards=(), held_as=jnp.bfloat16):
    array = deviation * jax.random.normal(rng, dims, jnp.float32)
    if shards:
        array = array * block_scale(rng, dims, shards, -0.22, 0.18)
    return jnp.clip(array, -bound, bound).astype(held_as)


def heavy_noise(rng, shape, scale, limit, pieces, heavy, kind=jnp.bfloat16):
    values = scale * jax.random.normal(rng, shape, jnp.float32)
    if pieces:
        values = values * block_scale(rng, shape, pieces, -0.22, 0.18)
    return jnp.clip(strengthened(values, jax.random.fold_in(rng, 3), *heavy), -limit, limit).astype(kind)


def setup_inputs(seed: int = 0) -> dict:
    seeds = jax.random.split(jax.random.key(seed), 10)
    return {
        "latents": draw_latents(jax.random.fold_in(seeds[9], 71), 0),
        "cache_one": scatter_about(seeds[1], (CHANNELS, 2, HEIGHT, WIDTH), 1.0, 4.0, ((0, 4), (2, 8))),
        "cache_two": scatter_about(seeds[2], (CHANNELS, 2, HEIGHT, WIDTH), 1.0, 4.0, ((0, 4), (2, 8))),
        "gain_one": jnp.clip(1.0 + 0.15 * jax.random.normal(seeds[3], (CHANNELS,), jnp.float32), 0.25, 1.75),
        "bias_one": jnp.clip(jax.random.uniform(seeds[4], (CHANNELS,), jnp.float32, -0.8, 0.8) * block_scale(seeds[4], (CHANNELS,), ((0, 4),), -0.4, 0.0), -0.8, 0.8),
        "weight_one": scatter_about(seeds[5], (3, 3, 3, CHANNELS, CHANNELS), (27 * CHANNELS) ** -0.5, 0.0546875, ((4, 4),)),
        "gain_two": jnp.clip(1.0 + 0.15 * jax.random.normal(seeds[6], (CHANNELS,), jnp.float32), 0.25, 1.75),
        "bias_two": jnp.clip(jax.random.uniform(seeds[7], (CHANNELS,), jnp.float32, -0.8, 0.8) * block_scale(seeds[7], (CHANNELS,), ((0, 4),), -0.4, 0.0), -0.8, 0.8),
        "weight_two": heavy_noise(seeds[8], (3, 3, 3, CHANNELS, CHANNELS), (27 * CHANNELS) ** -0.5, 0.0625, ((3, 4),), (3, 4, 4, 2.0)),
    }


epsilon = 1e-06

def group_silu(values, gain, bias):
    grouped = values.reshape(GROUPS, CHANNELS // GROUPS, FRAMES, HEIGHT, WIDTH)
    average = lax.optimization_barrier(jnp.mean(grouped, axis=(1, 2, 3, 4), keepdims=True))
    spread = lax.optimization_barrier(jnp.mean((grouped - average) ** 2, axis=(1, 2, 3, 4), keepdims=True))
    normed = ((grouped - average) * lax.rsqrt(spread + epsilon)).reshape(CHANNELS, FRAMES, HEIGHT, WIDTH)
    scaled = normed * gain[:, None, None, None] + bias[:, None, None, None]
    return jax.nn.silu(scaled).astype(jnp.bfloat16)

def convolve(cache, field, kernel):
    frames = jnp.concatenate([cache, field], axis=1).astype(jnp.float32)
    result = lax.conv_general_dilated(frames[None], kernel.astype(jnp.float32), (1, 1, 1), ((0, 0), (1, 1), (1, 1)), dimension_numbers=('NCDHW', 'DHWIO', 'NCDHW'), precision=lax.Precision.HIGHEST)
    return result[0]

def reference(latents, cache_one, cache_two, gain_one, bias_one, weight_one, gain_two, bias_two, weight_two):
    floats = latents.astype(jnp.float32)
    first = group_silu(floats, gain_one, bias_one)
    middle = convolve(cache_one, first, weight_one).astype(jnp.bfloat16)
    second = group_silu(middle.astype(jnp.float32), gain_two, bias_two)
    result = floats + convolve(cache_two, second, weight_two)
    return jnp.repeat(jnp.repeat(result, 2, axis=2), 2, axis=3)
```

```python
import functools

import jax
import jax.numpy as jnp
from jax import lax
from jax.experimental import pallas as pl
from jax.experimental.pallas import tpu as pltpu
from jax.sharding import PartitionSpec as P

CHANNELS = 512
GROUPS = 32
MESH = pl.DeviceIdType.MESH
F32 = jnp.float32
BF16 = jnp.bfloat16


epsilon = 1e-06


def padded(block, sides, width):
    for axis, dim in sides:
        count = lax.axis_size(axis)
        forward = [(i, i + 1) for i in range(count - 1)]
        backward = [(target, source) for source, target in forward]
        low = lax.ppermute(
            lax.slice_in_dim(block, block.shape[dim] - width, None, axis=dim), axis, forward
        )
        high = lax.ppermute(lax.slice_in_dim(block, 0, width, axis=dim), axis, backward)
        block = jnp.concatenate([low, block, high], axis=dim)
    return block


def group_silu(values, gain, bias):
    group_size = CHANNELS // GROUPS
    grouped = values.reshape(values.shape[0] // group_size, -1)
    sums, squares = lax.psum((jnp.sum(grouped, axis=1), jnp.sum(grouped * grouped, axis=1)), "rows")
    members = grouped.shape[1] * lax.axis_size("rows")
    average = sums / members
    spread = squares / members - average * average
    normed = ((grouped - average[:, None]) * lax.rsqrt(spread + epsilon)[:, None]).reshape(
        values.shape
    )
    scaled = normed * gain[:, None, None, None] + bias[:, None, None, None]
    return jax.nn.silu(scaled).astype(jnp.bfloat16)


def pad_rows(frames):
    return padded(frames, (("rows", 2),), 1)


def conv_block(frames, kernel):
    result = lax.conv_general_dilated(
        frames[None],
        kernel,
        (1, 1, 1),
        ((0, 0), (0, 0), (1, 1)),
        dimension_numbers=("NCDHW", "DHWIO", "NCDHW"),
        preferred_element_type=jnp.float32,
    )
    return result[0]


def gathered_conv(frames, kernel):
    channels = lax.all_gather(frames, "chan", axis=0, tiled=True)
    return conv_block(channels, kernel)


def plain_body(
    latents, cache_one, cache_two, gain_one, bias_one, weight_one, gain_two, bias_two, weight_two
):
    floats = latents.astype(jnp.float32)
    first = group_silu(floats, gain_one, bias_one)
    frames_one = pad_rows(jnp.concatenate([cache_one, first], axis=1))
    middle = gathered_conv(frames_one, weight_one).astype(jnp.bfloat16)
    second = group_silu(middle.astype(jnp.float32), gain_two, bias_two)
    frames_two = pad_rows(jnp.concatenate([cache_two, second], axis=1))
    columns = lax.all_to_all(weight_two, "chan", split_axis=4, concat_axis=3, tiled=True)
    result = floats + gathered_conv(frames_two, columns)
    return jnp.repeat(jnp.repeat(result, 2, axis=2), 2, axis=3)


def block_kernel(
    R, Z, CL, T, W,
    lat_ref, c1_ref, c2_ref, g1_ref, b1_ref, g2_ref, b2_ref, w1_hbm, w2_hbm,
    out_ref,
    tmp, lat_t, xa, xs1, acc1, part_out, part_in, mid, mid_in, x2, xs2, acc2,
    st1, st2, rs_out, rs_in, w1, w2,
    wsem, cs, cr, hs, hr, fs, fr, s1s, s1r, ps, pr, ms, mr, s2s, s2r, rss, rsr,
):
    row = lax.axis_index("rows")
    me = lax.axis_index("chan")
    M = T * W
    C2 = 2 * W
    has_up = row > 0
    has_down = row < R - 1

    barrier = pltpu.get_barrier_semaphore()
    for k in range(1, R):
        pl.semaphore_signal(barrier, inc=1, device_id={"rows": lax.rem(row + k, R)}, device_id_type=MESH)
    for k in range(1, Z):
        pl.semaphore_signal(barrier, inc=1, device_id={"chan": lax.rem(me + k, Z)}, device_id_type=MESH)

    w_copies = []
    for dt in range(3):
        for dh in range(3):
            w_copies.append(
                pltpu.make_async_copy(
                    w1_hbm.at[dt, dh], w1.at[dt, :, :, pl.ds(dh * CL, CL)], wsem.at[dt * 3 + dh]
                )
            )
    w2_copy = pltpu.make_async_copy(w2_hbm, w2, wsem.at[9])
    for copy in w_copies:
        copy.start()
    w2_copy.start()

    def to_chan(src, dst, send, recv, k):
        return pltpu.make_async_remote_copy(
            src_ref=src, dst_ref=dst, send_sem=send, recv_sem=recv,
            device_id={"chan": lax.rem(me + k, Z)}, device_id_type=MESH,
        )

    def to_row(src, dst, send, recv, k):
        return pltpu.make_async_remote_copy(
            src_ref=src, dst_ref=dst, send_sem=send, recv_sem=recv,
            device_id={"rows": lax.rem(row + k, R)}, device_id_type=MESH,
        )

    tmp[0 : 2 * CL, :] = c1_ref[...].astype(F32)
    for t in range(2):
        xa[0, t * W : (t + 1) * W, :] = tmp[pl.ds(t, CL, stride=2), :].T.astype(BF16)
    tmp[0 : 2 * CL, :] = c2_ref[...].astype(F32)
    for t in range(2):
        x2[1, t * W : (t + 1) * W, :] = tmp[pl.ds(t, CL, stride=2), :].T.astype(BF16)

    pl.semaphore_wait(barrier, R - 1 + Z - 1)

    caches = [
        to_chan(xa.at[0, 0:C2], xa.at[k, 0:C2], cs.at[k], cr.at[k], k) for k in range(1, Z)
    ]
    for copy in caches:
        copy.start()
    halo_down = to_row(x2.at[1, 0:C2], x2.at[0, 0:C2], hs.at[0], hr.at[0], 1)
    halo_up = to_row(x2.at[1, 0:C2], x2.at[2, 0:C2], hs.at[1], hr.at[1], R - 1)

    tmp[...] = lat_ref[...].astype(F32)
    for t in range(T):
        lat_t[t * W : (t + 1) * W, :] = tmp[pl.ds(t, CL, stride=T), :].T

    members = F32(R * M * (CHANNELS // GROUPS))
    gi = lax.broadcasted_iota(jnp.int32, (CL, CL), 0) // (CHANNELS // GROUPS)
    gj = lax.broadcasted_iota(jnp.int32, (CL, CL), 1) // (CHANNELS // GROUPS)
    same_group = (gi == gj).astype(F32)

    def share_stats(values, st, send, recv):
        sums = jnp.sum(values, axis=0, keepdims=True)
        squares = jnp.sum(values * values, axis=0, keepdims=True)
        which = lax.broadcasted_iota(jnp.int32, (8, CL), 0)
        st[0] = jnp.where(which == 0, sums, jnp.where(which == 1, squares, 0.0))
        copies = [to_row(st.at[0], st.at[k], send.at[k], recv.at[k], k) for k in range(1, R)]
        for copy in copies:
            copy.start()
        return copies

    def finish_stats(copies, st, g_ref, b_ref):
        for copy in copies:
            copy.wait_recv()
        total = st[0]
        for k in range(1, R):
            total = total + st[k]
        total = jnp.dot(
            total, same_group, preferred_element_type=F32, precision=lax.Precision.HIGHEST
        ) / members
        mean = total[0:1, :]
        spread = jnp.maximum(total[1:2, :] - mean * mean, 0.0)
        scale = lax.rsqrt(spread + epsilon) * g_ref[...]
        return mean, scale, b_ref[...]

    def normed(values, coefs):
        mean, scale, bias = coefs
        u = (values - mean) * scale + bias
        return (u / (1.0 + jnp.exp(-u))).astype(BF16)

    stats_one = share_stats(lat_t[...], st1, s1s, s1r)

    @pl.when(has_down)
    def _():
        halo_down.start()

    @pl.when(has_up)
    def _():
        halo_up.start()

    coefs = finish_stats(stats_one, st1, g1_ref, b1_ref)
    xa[0, C2:, :] = normed(lat_t[...], coefs)
    firsts = [to_chan(xa.at[0, C2:], xa.at[k, C2:], fs.at[k], fr.at[k], k) for k in range(1, Z)]
    for copy in firsts:
        copy.start()

    cell = lax.broadcasted_iota(jnp.int32, (C2 + M, CL), 0) % W

    def shifted(block, store):
        wide = block.astype(F32)
        left = jnp.where(cell == 0, 0.0, pltpu.roll(wide, 1, 0)).astype(BF16)
        right = jnp.where(cell == W - 1, 0.0, pltpu.roll(wide, C2 + M - 1, 0)).astype(BF16)
        store(0, left)
        store(1, block)
        store(2, right)

    for k in range(Z):
        if k > 0:
            caches[k - 1].wait_recv()
            firsts[k - 1].wait_recv()
        z = lax.rem(me - k + Z, Z)

        def store_one(dx, value):
            xs1[:, dx * CL : (dx + 1) * CL] = value

        shifted(xa[k], store_one)
        if k == 0:
            for copy in w_copies:
                copy.wait()
        for dt in range(3):
            base = pl.ds(pl.multiple_of(z * CL, CL), CL)
            rhs = jnp.concatenate([w1[dt, dx, base, :] for dx in range(3)], axis=0)
            term = jnp.dot(xs1[dt * W : dt * W + M, :], rhs, preferred_element_type=F32)
            if k == 0 and dt == 0:
                acc1[...] = term
            else:
                acc1[...] += term

    part_down = to_row(part_out.at[0], part_in.at[0], ps.at[0], pr.at[0], 1)
    part_up = to_row(part_out.at[1], part_in.at[1], ps.at[1], pr.at[1], R - 1)
    part_out[0] = acc1[:, 0:CL].astype(part_out.dtype)

    @pl.when(has_down)
    def _():
        part_down.start()

    part_out[1] = acc1[:, 2 * CL : 3 * CL].astype(part_out.dtype)

    @pl.when(has_up)
    def _():
        part_up.start()

    acc1[:, 0:CL] = acc1[:, CL : 2 * CL]

    @pl.when(has_up)
    def _():
        part_down.wait_recv()
        acc1[:, 0:CL] += part_in[0].astype(F32)

    @pl.when(has_down)
    def _():
        part_up.wait_recv()
        acc1[:, 0:CL] += part_in[1].astype(F32)

    mid[...] = acc1[:, 0:CL].astype(BF16)
    mid_down = to_row(mid, mid_in.at[0], ms.at[0], mr.at[0], 1)
    mid_up = to_row(mid, mid_in.at[1], ms.at[1], mr.at[1], R - 1)

    stats_two = share_stats(mid[...].astype(F32), st2, s2s, s2r)

    @pl.when(has_down)
    def _():
        mid_down.start()

    @pl.when(has_up)
    def _():
        mid_up.start()

    coefs_two = finish_stats(stats_two, st2, g2_ref, b2_ref)
    w2_copy.wait()

    def conv_two(dh, first):
        def store_two(dx, value):
            xs2[:, dx * CL : (dx + 1) * CL] = value

        shifted(x2[dh], store_two)
        for dt in range(3):
            lhs = xs2[dt * W : dt * W + M, :]
            term = jnp.dot(lhs, w2[dt, dh], preferred_element_type=F32)
            for d in range(Z):
                if first and dt == 0:
                    acc2[d] = term[:, d * CL : (d + 1) * CL]
                else:
                    acc2[d] += term[:, d * CL : (d + 1) * CL]

    x2[1, C2:, :] = normed(mid[...].astype(F32), coefs_two)
    conv_two(1, True)

    @pl.when(has_up)
    def _():
        halo_down.wait_recv()
        mid_down.wait_recv()
        x2[0, C2:, :] = normed(mid_in[0].astype(F32), coefs_two)
        conv_two(0, False)

    @pl.when(has_down)
    def _():
        halo_up.wait_recv()
        mid_up.wait_recv()
        x2[2, C2:, :] = normed(mid_in[1].astype(F32), coefs_two)
        conv_two(2, False)

    reduces = []
    for k in range(1, Z):
        rs_out[k - 1] = acc2[lax.rem(me + k, Z)].astype(rs_out.dtype)
        copy = to_chan(rs_out.at[k - 1], rs_in.at[k - 1], rss.at[k], rsr.at[k], k)
        copy.start()
        reduces.append(copy)
    lat_t[...] = lat_t[...] + acc2[me]
    for k in range(1, Z):
        reduces[k - 1].wait_recv()
        lat_t[...] += rs_in[k - 1].astype(F32)

    ei = lax.broadcasted_iota(jnp.int32, (W, 2 * W), 0)
    ej = lax.broadcasted_iota(jnp.int32, (W, 2 * W), 1) // 2
    twice = (ei == ej).astype(F32)
    for t in range(T):
        wide = jnp.dot(
            lat_t[t * W : (t + 1) * W, :].T, twice,
            preferred_element_type=F32, precision=lax.Precision.HIGHEST,
        )
        for half in range(2):
            for again in range(2):
                out_ref[pl.ds(t * 4 + half * 2 + again, CL, stride=4 * T), :] = wide[
                    :, half * W : (half + 1) * W
                ]

    for copy in caches + firsts + stats_one + stats_two + reduces:
        copy.wait_send()

    @pl.when(has_down)
    def _():
        for copy in (halo_down, part_down, mid_down):
            copy.wait_send()

    @pl.when(has_up)
    def _():
        for copy in (halo_up, part_up, mid_up):
            copy.wait_send()


def body(
    latents, cache_one, cache_two, gain_one, bias_one, weight_one, gain_two, bias_two, weight_two
):
    CL, T, rows_here, W = latents.shape
    R, Z = lax.axis_size("rows"), lax.axis_size("chan")
    if CL % 128 or W % 128 or rows_here != 1 or R < 2 or Z < 2:
        return plain_body(
            latents, cache_one, cache_two, gain_one, bias_one, weight_one, gain_two, bias_two,
            weight_two,
        )
    C = CL * Z
    M = T * W
    vmem = pl.BlockSpec(memory_space=pltpu.VMEM)
    anywhere = pl.BlockSpec(memory_space=pl.ANY)
    dma = pltpu.SemaphoreType.DMA
    out = pl.pallas_call(
        functools.partial(block_kernel, R, Z, CL, T, W),
        out_shape=jax.ShapeDtypeStruct((CL * T * 4, W), F32),
        in_specs=[vmem] * 7 + [anywhere] * 2,
        out_specs=vmem,
        scratch_shapes=[
            pltpu.VMEM((CL * T, W), F32),
            pltpu.VMEM((M, CL), F32),
            pltpu.VMEM((Z, M + 2 * W, CL), BF16),
            pltpu.VMEM((M + 2 * W, 3 * CL), BF16),
            pltpu.VMEM((M, 3 * CL), F32),
            pltpu.VMEM((2, M, CL), BF16),
            pltpu.VMEM((2, M, CL), BF16),
            pltpu.VMEM((M, CL), BF16),
            pltpu.VMEM((2, M, CL), BF16),
            pltpu.VMEM((3, M + 2 * W, CL), BF16),
            pltpu.VMEM((M + 2 * W, 3 * CL), BF16),
            pltpu.VMEM((Z, M, CL), F32),
            pltpu.VMEM((R, 8, CL), F32),
            pltpu.VMEM((R, 8, CL), F32),
            pltpu.VMEM((Z - 1, M, CL), BF16),
            pltpu.VMEM((Z - 1, M, CL), BF16),
            pltpu.VMEM((3, 3, C, 3 * CL), BF16),
            pltpu.VMEM((3, 3, 3 * CL, C), BF16),
            dma((10,)),
            dma((Z,)), dma((Z,)),
            dma((2,)), dma((2,)),
            dma((Z,)), dma((Z,)),
            dma((R,)), dma((R,)),
            dma((2,)), dma((2,)),
            dma((2,)), dma((2,)),
            dma((R,)), dma((R,)),
            dma((Z,)), dma((Z,)),
        ],
        compiler_params=pltpu.CompilerParams(
            collective_id=0, has_side_effects=True, vmem_limit_bytes=40 * 1024 * 1024
        ),
    )(
        latents.reshape(CL * T, W),
        cache_one.reshape(CL * 2, W),
        cache_two.reshape(CL * 2, W),
        gain_one.reshape(1, CL),
        bias_one.reshape(1, CL),
        gain_two.reshape(1, CL),
        bias_two.reshape(1, CL),
        weight_one,
        weight_two.reshape(3, 3, 3 * CL, C),
    )
    return out.reshape(CL, T, 2, 2, W).transpose(0, 1, 3, 2, 4).reshape(CL, T, 2, 2 * W)


def solution(mesh):
    return jax.shard_map(
        body,
        mesh=mesh,
        in_specs=(
            P("chan", None, "rows", None),
            P("chan", None, "rows", None),
            P("chan", None, "rows", None),
            P("chan"),
            P("chan"),
            P(None, None, None, None, "chan"),
            P("chan"),
            P("chan"),
            P(None, None, None, "chan", None),
        ),
        out_specs=P("chan", None, "rows", None),
        check_vma=False,
    )
```

```python
import functools

import jax
import jax.numpy as jnp
from jax import lax
from jax.experimental import pallas as pl
from jax.experimental.pallas import tpu as pltpu
from jax.sharding import PartitionSpec as P

CHANNELS = 512
GROUPS = 32
MESH = pl.DeviceIdType.MESH
F32 = jnp.float32
BF16 = jnp.bfloat16


epsilon = 1e-06


def padded(block, sides, width):
    for axis, dim in sides:
        count = lax.axis_size(axis)
        forward = [(i, i + 1) for i in range(count - 1)]
        backward = [(target, source) for source, target in forward]
        low = lax.ppermute(
            lax.slice_in_dim(block, block.shape[dim] - width, None, axis=dim), axis, forward
        )
        high = lax.ppermute(lax.slice_in_dim(block, 0, width, axis=dim), axis, backward)
        block = jnp.concatenate([low, block, high], axis=dim)
    return block


def group_silu(values, gain, bias):
    group_size = CHANNELS // GROUPS
    grouped = values.reshape(values.shape[0] // group_size, -1)
    sums, squares = lax.psum((jnp.sum(grouped, axis=1), jnp.sum(grouped * grouped, axis=1)), "rows")
    members = grouped.shape[1] * lax.axis_size("rows")
    average = sums / members
    spread = squares / members - average * average
    normed = ((grouped - average[:, None]) * lax.rsqrt(spread + epsilon)[:, None]).reshape(
        values.shape
    )
    scaled = normed * gain[:, None, None, None] + bias[:, None, None, None]
    return jax.nn.silu(scaled).astype(jnp.bfloat16)


def pad_rows(frames):
    return padded(frames, (("rows", 2),), 1)


def conv_block(frames, kernel):
    result = lax.conv_general_dilated(
        frames[None],
        kernel,
        (1, 1, 1),
        ((0, 0), (0, 0), (1, 1)),
        dimension_numbers=("NCDHW", "DHWIO", "NCDHW"),
        preferred_element_type=jnp.float32,
    )
    return result[0]


def gathered_conv(frames, kernel):
    channels = lax.all_gather(frames, "chan", axis=0, tiled=True)
    return conv_block(channels, kernel)


def plain_body(
    latents, cache_one, cache_two, gain_one, bias_one, weight_one, gain_two, bias_two, weight_two
):
    floats = latents.astype(jnp.float32)
    first = group_silu(floats, gain_one, bias_one)
    frames_one = pad_rows(jnp.concatenate([cache_one, first], axis=1))
    middle = gathered_conv(frames_one, weight_one).astype(jnp.bfloat16)
    second = group_silu(middle.astype(jnp.float32), gain_two, bias_two)
    frames_two = pad_rows(jnp.concatenate([cache_two, second], axis=1))
    columns = lax.all_to_all(weight_two, "chan", split_axis=4, concat_axis=3, tiled=True)
    result = floats + gathered_conv(frames_two, columns)
    return jnp.repeat(jnp.repeat(result, 2, axis=2), 2, axis=3)


def block_kernel(
    R, Z, CL, T, W,
    lat_hbm, c1_hbm, c2_hbm, g1_hbm, b1_hbm, g2_hbm, b2_hbm, w1_hbm, w2_hbm,
    out_ref,
    lat_v, c1_v, c2_v, g1, b1, g2, b2,
    tmp, lat_t, xa, xs1, acc1, part_out, part_in, mid, mid_in, x2, xs2, acc2,
    st1, st2, rs_out, rs_in, w1, w2,
    isem, wsem, cs, cr, hs, hr, fs, fr, s1s, s1r, ps, pr, ms, mr, s2s, s2r, rss, rsr,
):
    row = lax.axis_index("rows")
    me = lax.axis_index("chan")
    M = T * W
    C2 = 2 * W
    ZH = Z // 2
    H = M // 2
    has_up = row > 0
    has_down = row < R - 1

    def partner(k):
        other = me * 0
        bit = 1
        while bit < Z:
            mine = (me // bit) % 2
            other = other + bit * ((1 - mine) if k & bit else mine)
            bit *= 2
        return other

    barrier = pltpu.get_barrier_semaphore()
    for k in range(1, R):
        pl.semaphore_signal(barrier, inc=1, device_id={"rows": lax.rem(row + k, R)}, device_id_type=MESH)
    for k in range(1, Z):
        pl.semaphore_signal(barrier, inc=1, device_id={"chan": partner(k)}, device_id_type=MESH)

    loads = [
        pltpu.make_async_copy(src, dst, isem.at[i])
        for i, (src, dst) in enumerate(
            [
                (lat_hbm, lat_v), (c1_hbm, c1_v), (c2_hbm, c2_v),
                (g1_hbm, g1), (b1_hbm, b1), (g2_hbm, g2), (b2_hbm, b2),
            ]
        )
    ]
    place = (0, 2, 1)
    w_copies = []
    for dt in range(3):
        for dh in range(3):
            w_copies.append(
                pltpu.make_async_copy(
                    w1_hbm.at[dt, dh],
                    w1.at[dt, :, :, pl.ds(place[dh] * CL, CL)],
                    wsem.at[dt * 3 + dh],
                )
            )
    w2_copy = pltpu.make_async_copy(w2_hbm, w2, wsem.at[9])
    for copy in loads + w_copies + [w2_copy]:
        copy.start()

    def to_chan(src, dst, send, recv, k):
        return pltpu.make_async_remote_copy(
            src_ref=src, dst_ref=dst, send_sem=send, recv_sem=recv,
            device_id={"chan": partner(k)}, device_id_type=MESH,
        )

    def to_row(src, dst, send, recv, k):
        return pltpu.make_async_remote_copy(
            src_ref=src, dst_ref=dst, send_sem=send, recv_sem=recv,
            device_id={"rows": lax.rem(row + k, R)}, device_id_type=MESH,
        )

    members = F32(R * M * (CHANNELS // GROUPS))
    gi = lax.broadcasted_iota(jnp.int32, (CL, CL), 0) // (CHANNELS // GROUPS)
    gj = lax.broadcasted_iota(jnp.int32, (CL, CL), 1) // (CHANNELS // GROUPS)
    same_group = (gi == gj).astype(F32)

    def share_stats(values, st, send, recv):
        sums = jnp.sum(values, axis=0, keepdims=True)
        squares = jnp.sum(values * values, axis=0, keepdims=True)
        which = lax.broadcasted_iota(jnp.int32, (8, CL), 0)
        st[0] = jnp.where(which == 0, sums, jnp.where(which == 1, squares, 0.0))
        copies = [to_row(st.at[0], st.at[k], send.at[k], recv.at[k], k) for k in range(1, R)]
        for copy in copies:
            copy.start()
        return copies

    def finish_stats(copies, st, g_ref, b_ref):
        for copy in copies:
            copy.wait_recv()
        total = st[0]
        for k in range(1, R):
            total = total + st[k]
        total = jnp.dot(
            total, same_group, preferred_element_type=F32, precision=lax.Precision.HIGHEST
        ) / members
        mean = total[0:1, :]
        spread = jnp.maximum(total[1:2, :] - mean * mean, 0.0)
        scale = lax.rsqrt(spread + epsilon) * g_ref[...]
        return mean, scale, b_ref[...]

    def normed(values, coefs):
        mean, scale, bias = coefs
        u = (values - mean) * scale + bias
        return (u / (1.0 + jnp.exp(-u))).astype(BF16)

    def shifted(block):
        rows = block.shape[0]
        cell = lax.broadcasted_iota(jnp.int32, (rows, CL), 0) % W
        wide = block.astype(F32)
        left = jnp.where(cell == 0, 0.0, pltpu.roll(wide, 1, 0)).astype(BF16)
        right = jnp.where(cell == W - 1, 0.0, pltpu.roll(wide, rows - 1, 0)).astype(BF16)
        return left, block, right

    loads[0].wait()
    tmp[...] = lat_v[...].astype(F32)
    for t in range(T):
        lat_t[t * W : (t + 1) * W, :] = tmp[pl.ds(t, CL, stride=T), :].T
    loads[1].wait()
    tmp[0 : 2 * CL, :] = c1_v[...].astype(F32)
    for t in range(2):
        xa[0, t * W : (t + 1) * W, :] = tmp[pl.ds(t, CL, stride=2), :].T.astype(BF16)

    pl.semaphore_wait(barrier, R - 1 + Z - 1)

    stats_one = share_stats(lat_t[...], st1, s1s, s1r)
    caches = [
        to_chan(xa.at[0, 0:C2], xa.at[k, 0:C2], cs.at[k], cr.at[k], k) for k in range(1, Z)
    ]
    for copy in caches[::-1]:
        copy.start()

    loads[2].wait()
    tmp[0 : 2 * CL, :] = c2_v[...].astype(F32)
    for t in range(2):
        x2[1, t * W : (t + 1) * W, :] = tmp[pl.ds(t, CL, stride=2), :].T.astype(BF16)
    halo_down = to_row(x2.at[1], x2.at[0], hs.at[0], hr.at[0], 1)
    halo_up = to_row(x2.at[1], x2.at[2], hs.at[1], hr.at[1], R - 1)

    @pl.when(has_down)
    def _():
        halo_down.start()

    @pl.when(has_up)
    def _():
        halo_up.start()

    for copy in loads[3:]:
        copy.wait()
    coefs = finish_stats(stats_one, st1, g1, b1)
    xa[0, C2:, :] = normed(lat_t[...], coefs)
    firsts = [to_chan(xa.at[0, C2:], xa.at[k, C2:], fs.at[k], fr.at[k], k) for k in range(1, Z)]
    for copy in firsts[::-1]:
        copy.start()

    part_down = to_row(part_out.at[0], part_in.at[0], ps.at[0], pr.at[0], 1)
    part_up = to_row(part_out.at[1], part_in.at[1], ps.at[1], pr.at[1], R - 1)

    def kernel_one(dt, z, low, high):
        base = pl.ds(pl.multiple_of(z * CL, CL), CL)
        return jnp.concatenate([w1[dt, dx, base, low:high] for dx in range(3)], axis=0)

    for copy in w_copies:
        copy.wait()
    for k in range(Z):
        if k > 0:
            caches[k - 1].wait_recv()
            firsts[k - 1].wait_recv()
        z = partner(k)
        for dx, value in enumerate(shifted(xa[k])):
            xs1[:, dx * CL : (dx + 1) * CL] = value
        parts = ((0, 2 * CL), (2 * CL, 3 * CL)) if k == Z - 1 else ((0, 3 * CL),)
        for low, high in parts:
            for dt in range(3):
                term = jnp.dot(
                    xs1[dt * W : dt * W + M, :], kernel_one(dt, z, low, high),
                    preferred_element_type=F32,
                )
                if k == 0 and dt == 0:
                    acc1[:, low:high] = term
                else:
                    acc1[:, low:high] += term
            if k == Z - 1 and low == 0:
                part_out[0] = acc1[:, 0:CL].astype(part_out.dtype)
                part_out[1] = acc1[:, CL : 2 * CL].astype(part_out.dtype)

                @pl.when(has_down)
                def _():
                    part_down.start()

                @pl.when(has_up)
                def _():
                    part_up.start()

        if k == 0:
            w2_copy.wait()

            @pl.when(has_up)
            def _():
                halo_down.wait_recv()

            @pl.when(has_down)
            def _():
                halo_up.wait_recv()

            @pl.when(jnp.logical_not(has_up))
            def _():
                x2[0] = jnp.zeros((C2, CL), BF16)

            @pl.when(jnp.logical_not(has_down))
            def _():
                x2[2] = jnp.zeros((C2, CL), BF16)

            for dh in range(3):
                for dx, value in enumerate(shifted(x2[dh])):
                    xs2[0:C2, (dh * 3 + dx) * CL : (dh * 3 + dx + 1) * CL] = value
            both = jnp.dot(xs2[0:C2, :], w2[0], preferred_element_type=F32)
            one = jnp.dot(xs2[W:C2, :], w2[1], preferred_element_type=F32)
            for d in range(Z):
                cols = slice(d * CL, (d + 1) * CL)
                acc2[d, 0:W] = both[0:W, cols] + one[:, cols]
                acc2[d, W:C2] = both[W:C2, cols]
                acc2[d, C2:] = jnp.zeros((M - C2, CL), F32)

    @pl.when(has_up)
    def _():
        part_down.wait_recv()
        acc1[:, 2 * CL :] += part_in[0].astype(F32)

    @pl.when(has_down)
    def _():
        part_up.wait_recv()
        acc1[:, 2 * CL :] += part_in[1].astype(F32)

    mid[...] = acc1[:, 2 * CL :].astype(BF16)
    mid_down = to_row(mid, mid_in.at[0], ms.at[0], mr.at[0], 1)
    mid_up = to_row(mid, mid_in.at[1], ms.at[1], mr.at[1], R - 1)

    @pl.when(has_down)
    def _():
        mid_down.start()

    @pl.when(has_up)
    def _():
        mid_up.start()

    stats_two = share_stats(mid[...].astype(F32), st2, s2s, s2r)
    coefs_two = finish_stats(stats_two, st2, g2, b2)

    def place_row(dh, values):
        for dx, value in enumerate(shifted(normed(values.astype(F32), coefs_two))):
            xs2[C2:, (dh * 3 + dx) * CL : (dh * 3 + dx + 1) * CL] = value

    place_row(1, mid[...])

    @pl.when(has_up)
    def _():
        mid_down.wait_recv()
        place_row(0, mid_in[0])

    @pl.when(has_down)
    def _():
        mid_up.wait_recv()
        place_row(2, mid_in[1])

    @pl.when(jnp.logical_not(has_up))
    def _():
        xs2[C2:, 0 : 3 * CL] = jnp.zeros((M, 3 * CL), BF16)

    @pl.when(jnp.logical_not(has_down))
    def _():
        xs2[C2:, 6 * CL :] = jnp.zeros((M, 3 * CL), BF16)

    mine = me // ZH
    reduces = {}
    for turn in range(2):
        half = 1 - mine if turn == 0 else mine
        cols = pl.ds(pl.multiple_of(half * (ZH * CL), ZH * CL), ZH * CL)
        for dt in (2, 1, 0):
            start = C2 - dt * W
            term = jnp.dot(
                xs2[C2 : C2 + M - start, :], w2[dt, :, cols], preferred_element_type=F32
            )
            for j in range(ZH):
                acc2[half * ZH + j, start:] += term[:, j * CL : (j + 1) * CL]
        ks = range(ZH, Z) if turn == 0 else range(1, ZH)
        for f in range(2):
            rows = slice(f * H, (f + 1) * H)
            for k in ks:
                rs_out[k - 1, rows] = acc2[partner(k), rows].astype(rs_out.dtype)
                copy = to_chan(
                    rs_out.at[k - 1, rows], rs_in.at[k - 1, rows], rss.at[f, k], rsr.at[f, k], k
                )
                copy.start()
                reduces[f, k] = copy
    lat_t[...] = lat_t[...] + acc2[me]

    ei = lax.broadcasted_iota(jnp.int32, (W, 2 * W), 0)
    ej = lax.broadcasted_iota(jnp.int32, (W, 2 * W), 1) // 2
    twice = (ei == ej).astype(F32)
    for f in range(2):
        for k in range(1, Z):
            reduces[f, k].wait_recv()
        for t in range(f * T // 2, (f + 1) * T // 2):
            rows = slice(t * W, (t + 1) * W)
            total = lat_t[rows, :]
            for k in range(1, Z):
                total = total + rs_in[k - 1, rows].astype(F32)
            wide = jnp.dot(
                total.T, twice, preferred_element_type=F32, precision=lax.Precision.HIGHEST
            )
            for side in range(2):
                for again in range(2):
                    out_ref[pl.ds(t * 4 + side * 2 + again, CL, stride=4 * T), :] = wide[
                        :, side * W : (side + 1) * W
                    ]

    for copy in caches + firsts + stats_one + stats_two + list(reduces.values()):
        copy.wait_send()

    @pl.when(has_down)
    def _():
        for copy in (halo_down, part_down, mid_down):
            copy.wait_send()

    @pl.when(has_up)
    def _():
        for copy in (halo_up, part_up, mid_up):
            copy.wait_send()


def body(
    latents, cache_one, cache_two, gain_one, bias_one, weight_one, gain_two, bias_two, weight_two
):
    CL, T, rows_here, W = latents.shape
    R, Z = lax.axis_size("rows"), lax.axis_size("chan")
    if CL % 128 or W % 128 or rows_here != 1 or T % 2 or R < 2 or Z < 2 or Z & (Z - 1):
        return plain_body(
            latents, cache_one, cache_two, gain_one, bias_one, weight_one, gain_two, bias_two,
            weight_two,
        )
    C = CL * Z
    M = T * W
    vmem = pl.BlockSpec(memory_space=pltpu.VMEM)
    hbm = pl.BlockSpec(memory_space=pltpu.HBM)
    dma = pltpu.SemaphoreType.DMA
    out = pl.pallas_call(
        functools.partial(block_kernel, R, Z, CL, T, W),
        out_shape=jax.ShapeDtypeStruct((CL * T * 4, W), F32),
        in_specs=[hbm] * 9,
        out_specs=vmem,
        scratch_shapes=[
            pltpu.VMEM((CL * T, W), BF16),
            pltpu.VMEM((CL * 2, W), BF16),
            pltpu.VMEM((CL * 2, W), BF16),
            pltpu.VMEM((1, CL), F32),
            pltpu.VMEM((1, CL), F32),
            pltpu.VMEM((1, CL), F32),
            pltpu.VMEM((1, CL), F32),
            pltpu.VMEM((CL * T, W), F32),
            pltpu.VMEM((M, CL), F32),
            pltpu.VMEM((Z, M + 2 * W, CL), BF16),
            pltpu.VMEM((M + 2 * W, 3 * CL), BF16),
            pltpu.VMEM((M, 3 * CL), F32),
            pltpu.VMEM((2, M, CL), BF16),
            pltpu.VMEM((2, M, CL), BF16),
            pltpu.VMEM((M, CL), BF16),
            pltpu.VMEM((2, M, CL), BF16),
            pltpu.VMEM((3, 2 * W, CL), BF16),
            pltpu.VMEM((M + 2 * W, 9 * CL), BF16),
            pltpu.VMEM((Z, M, CL), F32),
            pltpu.VMEM((R, 8, CL), F32),
            pltpu.VMEM((R, 8, CL), F32),
            pltpu.VMEM((Z - 1, M, CL), BF16),
            pltpu.VMEM((Z - 1, M, CL), BF16),
            pltpu.VMEM((3, 3, C, 3 * CL), BF16),
            pltpu.VMEM((3, 9 * CL, C), BF16),
            dma((7,)),
            dma((10,)),
            dma((Z,)), dma((Z,)),
            dma((2,)), dma((2,)),
            dma((Z,)), dma((Z,)),
            dma((R,)), dma((R,)),
            dma((2,)), dma((2,)),
            dma((2,)), dma((2,)),
            dma((R,)), dma((R,)),
            dma((2, Z)), dma((2, Z)),
        ],
        compiler_params=pltpu.CompilerParams(
            collective_id=0, has_side_effects=True, vmem_limit_bytes=60 * 1024 * 1024
        ),
    )(
        latents.reshape(CL * T, W),
        cache_one.reshape(CL * 2, W),
        cache_two.reshape(CL * 2, W),
        gain_one.reshape(1, CL),
        bias_one.reshape(1, CL),
        gain_two.reshape(1, CL),
        bias_two.reshape(1, CL),
        weight_one,
        weight_two.reshape(3, 9 * CL, C),
    )
    return out.reshape(CL, T, 2, 2, W).transpose(0, 1, 3, 2, 4).reshape(CL, T, 2, 2 * W)


def solution(mesh):
    return jax.shard_map(
        body,
        mesh=mesh,
        in_specs=(
            P("chan", None, "rows", None),
            P("chan", None, "rows", None),
            P("chan", None, "rows", None),
            P("chan"),
            P("chan"),
            P(None, None, None, None, "chan"),
            P("chan"),
            P("chan"),
            P(None, None, None, "chan", None),
        ),
        out_specs=P("chan", None, "rows", None),
        check_vma=False,
    )
```

```python
import functools

import jax
import jax.numpy as jnp
from jax import lax
from jax.experimental import pallas as pl
from jax.experimental.pallas import tpu as pltpu
from jax.sharding import PartitionSpec as P

CHANNELS = 512
GROUPS = 32
MESH = pl.DeviceIdType.MESH
F32 = jnp.float32
BF16 = jnp.bfloat16


epsilon = 1e-06


def padded(block, sides, width):
    for axis, dim in sides:
        count = lax.axis_size(axis)
        forward = [(i, i + 1) for i in range(count - 1)]
        backward = [(target, source) for source, target in forward]
        low = lax.ppermute(
            lax.slice_in_dim(block, block.shape[dim] - width, None, axis=dim), axis, forward
        )
        high = lax.ppermute(lax.slice_in_dim(block, 0, width, axis=dim), axis, backward)
        block = jnp.concatenate([low, block, high], axis=dim)
    return block


def group_silu(values, gain, bias):
    group_size = CHANNELS // GROUPS
    grouped = values.reshape(values.shape[0] // group_size, -1)
    sums, squares = lax.psum((jnp.sum(grouped, axis=1), jnp.sum(grouped * grouped, axis=1)), "rows")
    members = grouped.shape[1] * lax.axis_size("rows")
    average = sums / members
    spread = squares / members - average * average
    normed = ((grouped - average[:, None]) * lax.rsqrt(spread + epsilon)[:, None]).reshape(
        values.shape
    )
    scaled = normed * gain[:, None, None, None] + bias[:, None, None, None]
    return jax.nn.silu(scaled).astype(jnp.bfloat16)


def pad_rows(frames):
    return padded(frames, (("rows", 2),), 1)


def conv_block(frames, kernel):
    result = lax.conv_general_dilated(
        frames[None],
        kernel,
        (1, 1, 1),
        ((0, 0), (0, 0), (1, 1)),
        dimension_numbers=("NCDHW", "DHWIO", "NCDHW"),
        preferred_element_type=jnp.float32,
    )
    return result[0]


def gathered_conv(frames, kernel):
    channels = lax.all_gather(frames, "chan", axis=0, tiled=True)
    return conv_block(channels, kernel)


def plain_body(
    latents, cache_one, cache_two, gain_one, bias_one, weight_one, gain_two, bias_two, weight_two
):
    floats = latents.astype(jnp.float32)
    first = group_silu(floats, gain_one, bias_one)
    frames_one = pad_rows(jnp.concatenate([cache_one, first], axis=1))
    middle = gathered_conv(frames_one, weight_one).astype(jnp.bfloat16)
    second = group_silu(middle.astype(jnp.float32), gain_two, bias_two)
    frames_two = pad_rows(jnp.concatenate([cache_two, second], axis=1))
    columns = lax.all_to_all(weight_two, "chan", split_axis=4, concat_axis=3, tiled=True)
    result = floats + gathered_conv(frames_two, columns)
    return jnp.repeat(jnp.repeat(result, 2, axis=2), 2, axis=3)


def block_kernel(
    R, Z, CL, T, W,
    lat_hbm, c1_hbm, c2_hbm, g1_hbm, b1_hbm, g2_hbm, b2_hbm, w1_hbm, w2_hbm,
    out_ref,
    lat_v, c1_v, c2_v, g1, b1, g2, b2,
    tmp, lat_t, xa, xs1, acc1, part_out, part_in, mid, mid_in, x2, xs2, acc2,
    st1, st2, rs_out, rs_in, w1, w2,
    isem, wsem, cs, cr, hs, hr, fs, fr, s1s, s1r, ps, pr, ms, mr, s2s, s2r, rss, rsr,
):
    row = lax.axis_index("rows")
    me = lax.axis_index("chan")
    M = T * W
    C2 = 2 * W
    ZH = Z // 2
    H = M // 2
    has_up = row > 0
    has_down = row < R - 1

    def partner(k):
        other = me * 0
        bit = 1
        while bit < Z:
            mine = (me // bit) % 2
            other = other + bit * ((1 - mine) if k & bit else mine)
            bit *= 2
        return other

    barrier = pltpu.get_barrier_semaphore()
    for k in range(1, R):
        pl.semaphore_signal(barrier, inc=1, device_id={"rows": lax.rem(row + k, R)}, device_id_type=MESH)
    for k in range(1, Z):
        pl.semaphore_signal(barrier, inc=1, device_id={"chan": partner(k)}, device_id_type=MESH)

    loads = [
        pltpu.make_async_copy(src, dst, isem.at[i])
        for i, (src, dst) in enumerate(
            [
                (lat_hbm, lat_v), (c1_hbm, c1_v), (c2_hbm, c2_v),
                (g1_hbm, g1), (b1_hbm, b1), (g2_hbm, g2), (b2_hbm, b2),
            ]
        )
    ]
    place = (0, 2, 1)
    w_copies = []
    for dt in range(3):
        for dh in range(3):
            w_copies.append(
                pltpu.make_async_copy(
                    w1_hbm.at[dt, dh],
                    w1.at[dt, :, :, pl.ds(place[dh] * CL, CL)],
                    wsem.at[dt * 3 + dh],
                )
            )
    w2_copy = pltpu.make_async_copy(w2_hbm, w2, wsem.at[9])
    for copy in loads + w_copies + [w2_copy]:
        copy.start()

    def to_chan(src, dst, send, recv, k):
        return pltpu.make_async_remote_copy(
            src_ref=src, dst_ref=dst, send_sem=send, recv_sem=recv,
            device_id={"chan": partner(k)}, device_id_type=MESH,
        )

    def to_row(src, dst, send, recv, k):
        return pltpu.make_async_remote_copy(
            src_ref=src, dst_ref=dst, send_sem=send, recv_sem=recv,
            device_id={"rows": lax.rem(row + k, R)}, device_id_type=MESH,
        )

    members = F32(R * M * (CHANNELS // GROUPS))
    gi = lax.broadcasted_iota(jnp.int32, (CL, CL), 0) // (CHANNELS // GROUPS)
    gj = lax.broadcasted_iota(jnp.int32, (CL, CL), 1) // (CHANNELS // GROUPS)
    same_group = (gi == gj).astype(F32)

    def share_stats(values, st, send, recv):
        sums = jnp.sum(values, axis=0, keepdims=True)
        squares = jnp.sum(values * values, axis=0, keepdims=True)
        which = lax.broadcasted_iota(jnp.int32, (8, CL), 0)
        st[0] = jnp.where(which == 0, sums, jnp.where(which == 1, squares, 0.0))
        copies = [to_row(st.at[0], st.at[k], send.at[k], recv.at[k], k) for k in range(1, R)]
        for copy in copies:
            copy.start()
        return copies

    def finish_stats(copies, st, g_ref, b_ref):
        for copy in copies:
            copy.wait_recv()
        total = st[0]
        for k in range(1, R):
            total = total + st[k]
        total = jnp.dot(
            total, same_group, preferred_element_type=F32, precision=lax.Precision.HIGHEST
        ) / members
        mean = total[0:1, :]
        spread = jnp.maximum(total[1:2, :] - mean * mean, 0.0)
        scale = lax.rsqrt(spread + epsilon) * g_ref[...]
        return mean, scale, b_ref[...]

    def normed(values, coefs):
        mean, scale, bias = coefs
        u = (values - mean) * scale + bias
        return (u / (1.0 + jnp.exp(-u))).astype(BF16)

    def shifted(block):
        rows = block.shape[0]
        cell = lax.broadcasted_iota(jnp.int32, (rows, CL), 0) % W
        wide = block.astype(F32)
        left = jnp.where(cell == 0, 0.0, pltpu.roll(wide, 1, 0)).astype(BF16)
        right = jnp.where(cell == W - 1, 0.0, pltpu.roll(wide, rows - 1, 0)).astype(BF16)
        return left, block, right

    loads[0].wait()
    tmp[...] = lat_v[...].astype(F32)
    for t in range(T):
        lat_t[t * W : (t + 1) * W, :] = tmp[pl.ds(t, CL, stride=T), :].T
    loads[1].wait()
    tmp[0 : 2 * CL, :] = c1_v[...].astype(F32)
    for t in range(2):
        xa[0, t * W : (t + 1) * W, :] = tmp[pl.ds(t, CL, stride=2), :].T.astype(BF16)

    pl.semaphore_wait(barrier, R - 1 + Z - 1)

    stats_one = share_stats(lat_t[...], st1, s1s, s1r)
    caches = [
        to_chan(xa.at[0, 0:C2], xa.at[k, 0:C2], cs.at[k], cr.at[k], k) for k in range(1, Z)
    ]
    for copy in caches[::-1]:
        copy.start()

    loads[2].wait()
    tmp[0 : 2 * CL, :] = c2_v[...].astype(F32)
    for t in range(2):
        x2[1, t * W : (t + 1) * W, :] = tmp[pl.ds(t, CL, stride=2), :].T.astype(BF16)
    halo_down = to_row(x2.at[1], x2.at[0], hs.at[0], hr.at[0], 1)
    halo_up = to_row(x2.at[1], x2.at[2], hs.at[1], hr.at[1], R - 1)

    @pl.when(has_down)
    def _():
        halo_down.start()

    @pl.when(has_up)
    def _():
        halo_up.start()

    for copy in loads[3:]:
        copy.wait()
    coefs = finish_stats(stats_one, st1, g1, b1)
    xa[0, C2:, :] = normed(lat_t[...], coefs)
    firsts = [to_chan(xa.at[0, C2:], xa.at[k, C2:], fs.at[k], fr.at[k], k) for k in range(1, Z)]
    for copy in firsts[::-1]:
        copy.start()

    part_down = to_row(part_out.at[0], part_in.at[0], ps.at[0], pr.at[0], 1)
    part_up = to_row(part_out.at[1], part_in.at[1], ps.at[1], pr.at[1], R - 1)

    def kernel_one(dt, z, low, high):
        base = pl.ds(pl.multiple_of(z * CL, CL), CL)
        return jnp.concatenate([w1[dt, dx, base, low:high] for dx in range(3)], axis=0)

    for copy in w_copies:
        copy.wait()
    for k in range(Z):
        if k > 0:
            caches[k - 1].wait_recv()
            firsts[k - 1].wait_recv()
        z = partner(k)
        for dx, value in enumerate(shifted(xa[k])):
            xs1[:, dx * CL : (dx + 1) * CL] = value
        parts = ((0, 2 * CL), (2 * CL, 3 * CL)) if k == Z - 1 else ((0, 3 * CL),)
        for low, high in parts:
            for dt in range(3):
                term = jnp.dot(
                    xs1[dt * W : dt * W + M, :], kernel_one(dt, z, low, high),
                    preferred_element_type=F32,
                )
                if k == 0 and dt == 0:
                    acc1[:, low:high] = term
                else:
                    acc1[:, low:high] += term
            if k == Z - 1 and low == 0:
                part_out[0] = acc1[:, 0:CL].astype(part_out.dtype)
                part_out[1] = acc1[:, CL : 2 * CL].astype(part_out.dtype)

                @pl.when(has_down)
                def _():
                    part_down.start()

                @pl.when(has_up)
                def _():
                    part_up.start()

        if k == 0:
            w2_copy.wait()

            @pl.when(has_up)
            def _():
                halo_down.wait_recv()

            @pl.when(has_down)
            def _():
                halo_up.wait_recv()

            @pl.when(jnp.logical_not(has_up))
            def _():
                x2[0] = jnp.zeros((C2, CL), BF16)

            @pl.when(jnp.logical_not(has_down))
            def _():
                x2[2] = jnp.zeros((C2, CL), BF16)

            for dh in range(3):
                for dx, value in enumerate(shifted(x2[dh])):
                    xs2[0:C2, (dh * 3 + dx) * CL : (dh * 3 + dx + 1) * CL] = value
            both = jnp.dot(xs2[0:C2, :], w2[0], preferred_element_type=F32)
            one = jnp.dot(xs2[W:C2, :], w2[1], preferred_element_type=F32)
            for d in range(Z):
                cols = slice(d * CL, (d + 1) * CL)
                acc2[d, 0:W] = both[0:W, cols] + one[:, cols]
                acc2[d, W:C2] = both[W:C2, cols]
                acc2[d, C2:] = jnp.zeros((M - C2, CL), F32)

    @pl.when(has_up)
    def _():
        part_down.wait_recv()
        acc1[:, 2 * CL :] += part_in[0].astype(F32)

    @pl.when(has_down)
    def _():
        part_up.wait_recv()
        acc1[:, 2 * CL :] += part_in[1].astype(F32)

    mid[...] = acc1[:, 2 * CL :].astype(BF16)
    mid_down = to_row(mid, mid_in.at[0], ms.at[0], mr.at[0], 1)
    mid_up = to_row(mid, mid_in.at[1], ms.at[1], mr.at[1], R - 1)

    @pl.when(has_down)
    def _():
        mid_down.start()

    @pl.when(has_up)
    def _():
        mid_up.start()

    stats_two = share_stats(mid[...].astype(F32), st2, s2s, s2r)
    coefs_two = finish_stats(stats_two, st2, g2, b2)

    def place_row(dh, values):
        for dx, value in enumerate(shifted(normed(values.astype(F32), coefs_two))):
            xs2[C2:, (dh * 3 + dx) * CL : (dh * 3 + dx + 1) * CL] = value

    place_row(1, mid[...])

    @pl.when(has_up)
    def _():
        mid_down.wait_recv()
        place_row(0, mid_in[0])

    @pl.when(has_down)
    def _():
        mid_up.wait_recv()
        place_row(2, mid_in[1])

    @pl.when(jnp.logical_not(has_up))
    def _():
        xs2[C2:, 0 : 3 * CL] = jnp.zeros((M, 3 * CL), BF16)

    @pl.when(jnp.logical_not(has_down))
    def _():
        xs2[C2:, 6 * CL :] = jnp.zeros((M, 3 * CL), BF16)

    mine = me // ZH
    reduces = {}
    for turn in range(2):
        half = 1 - mine if turn == 0 else mine
        cols = pl.ds(pl.multiple_of(half * (ZH * CL), ZH * CL), ZH * CL)
        for dt in (2, 1, 0):
            start = C2 - dt * W
            term = jnp.dot(
                xs2[C2 : C2 + M - start, :], w2[dt, :, cols], preferred_element_type=F32
            )
            for j in range(ZH):
                acc2[half * ZH + j, start:] += term[:, j * CL : (j + 1) * CL]
        ks = range(ZH, Z) if turn == 0 else range(1, ZH)
        for f in range(2):
            rows = slice(f * H, (f + 1) * H)
            for k in ks:
                rs_out[k - 1, rows] = acc2[partner(k), rows].astype(rs_out.dtype)
                copy = to_chan(
                    rs_out.at[k - 1, rows], rs_in.at[k - 1, rows], rss.at[f, k], rsr.at[f, k], k
                )
                copy.start()
                reduces[f, k] = copy
    lat_t[...] = lat_t[...] + acc2[me]

    ei = lax.broadcasted_iota(jnp.int32, (W, 2 * W), 0)
    ej = lax.broadcasted_iota(jnp.int32, (W, 2 * W), 1) // 2
    twice = (ei == ej).astype(F32)
    for f in range(2):
        for k in range(1, Z):
            reduces[f, k].wait_recv()
        for t in range(f * T // 2, (f + 1) * T // 2):
            rows = slice(t * W, (t + 1) * W)
            total = lat_t[rows, :]
            for k in range(1, Z):
                total = total + rs_in[k - 1, rows].astype(F32)
            wide = jnp.dot(
                total.T, twice, preferred_element_type=F32, precision=lax.Precision.HIGHEST
            )
            for side in range(2):
                for again in range(2):
                    out_ref[pl.ds(t * 4 + side * 2 + again, CL, stride=4 * T), :] = wide[
                        :, side * W : (side + 1) * W
                    ]

    for copy in caches + firsts + stats_one + stats_two + list(reduces.values()):
        copy.wait_send()

    @pl.when(has_down)
    def _():
        for copy in (halo_down, part_down, mid_down):
            copy.wait_send()

    @pl.when(has_up)
    def _():
        for copy in (halo_up, part_up, mid_up):
            copy.wait_send()


def body(
    latents, cache_one, cache_two, gain_one, bias_one, weight_one, gain_two, bias_two, weight_two
):
    CL, T, rows_here, W = latents.shape
    R, Z = lax.axis_size("rows"), lax.axis_size("chan")
    if CL % 128 or W % 128 or rows_here != 1 or T % 2 or R < 2 or Z < 2 or Z & (Z - 1):
        return plain_body(
            latents, cache_one, cache_two, gain_one, bias_one, weight_one, gain_two, bias_two,
            weight_two,
        )
    C = CL * Z
    M = T * W
    vmem = pl.BlockSpec(memory_space=pltpu.VMEM)
    hbm = pl.BlockSpec(memory_space=pltpu.HBM)
    dma = pltpu.SemaphoreType.DMA
    out = pl.pallas_call(
        functools.partial(block_kernel, R, Z, CL, T, W),
        out_shape=jax.ShapeDtypeStruct((CL * T * 4, W), F32),
        in_specs=[hbm] * 9,
        out_specs=vmem,
        scratch_shapes=[
            pltpu.VMEM((CL * T, W), BF16),
            pltpu.VMEM((CL * 2, W), BF16),
            pltpu.VMEM((CL * 2, W), BF16),
            pltpu.VMEM((1, CL), F32),
            pltpu.VMEM((1, CL), F32),
            pltpu.VMEM((1, CL), F32),
            pltpu.VMEM((1, CL), F32),
            pltpu.VMEM((CL * T, W), F32),
            pltpu.VMEM((M, CL), F32),
            pltpu.VMEM((Z, M + 2 * W, CL), BF16),
            pltpu.VMEM((M + 2 * W, 3 * CL), BF16),
            pltpu.VMEM((M, 3 * CL), F32),
            pltpu.VMEM((2, M, CL), BF16),
            pltpu.VMEM((2, M, CL), BF16),
            pltpu.VMEM((M, CL), BF16),
            pltpu.VMEM((2, M, CL), BF16),
            pltpu.VMEM((3, 2 * W, CL), BF16),
            pltpu.VMEM((M + 2 * W, 9 * CL), BF16),
            pltpu.VMEM((Z, M, CL), F32),
            pltpu.VMEM((R, 8, CL), F32),
            pltpu.VMEM((R, 8, CL), F32),
            pltpu.VMEM((Z - 1, M, CL), BF16),
            pltpu.VMEM((Z - 1, M, CL), BF16),
            pltpu.VMEM((3, 3, C, 3 * CL), BF16),
            pltpu.VMEM((3, 9 * CL, C), BF16),
            dma((7,)),
            dma((10,)),
            dma((Z,)), dma((Z,)),
            dma((2,)), dma((2,)),
            dma((Z,)), dma((Z,)),
            dma((R,)), dma((R,)),
            dma((2,)), dma((2,)),
            dma((2,)), dma((2,)),
            dma((R,)), dma((R,)),
            dma((2, Z)), dma((2, Z)),
        ],
        compiler_params=pltpu.CompilerParams(
            collective_id=0, has_side_effects=True, vmem_limit_bytes=40 * 1024 * 1024
        ),
    )(*(pltpu.with_memory_space_constraint(v, pltpu.HBM) for v in (
        latents.reshape(CL * T, W),
        cache_one.reshape(CL * 2, W),
        cache_two.reshape(CL * 2, W),
        gain_one.reshape(1, CL),
        bias_one.reshape(1, CL),
        gain_two.reshape(1, CL),
        bias_two.reshape(1, CL),
        weight_one,
        weight_two.reshape(3, 9 * CL, C),
    )))
    return out.reshape(CL, T, 2, 2, W).transpose(0, 1, 3, 2, 4).reshape(CL, T, 2, 2 * W)


def solution(mesh):
    return jax.shard_map(
        body,
        mesh=mesh,
        in_specs=(
            P("chan", None, "rows", None),
            P("chan", None, "rows", None),
            P("chan", None, "rows", None),
            P("chan"),
            P("chan"),
            P(None, None, None, None, "chan"),
            P("chan"),
            P("chan"),
            P(None, None, None, "chan", None),
        ),
        out_specs=P("chan", None, "rows", None),
        check_vma=False,
    )
```
